32 devices in a mesh: dp: 8 (over z, y), grp: 4 (over x, core).
Axes of the slice: x: 2, y: 2, z: 4, core: 2. Of those that a mesh axis runs over, the one named last changes fastest.
Arguments:
- clips: bfloat16 [8192, 1024], P(('dp', 'grp')), may hold values from -6 to 6
- captions: bfloat16 [128, 1024], P(('dp', 'grp')), may hold values from -6 to 6
- clip_group: int32 [8192], P(('dp', 'grp')), may hold values from 0 to 31, as said below
- caption_group: int32 [128], P(('dp', 'grp')), may hold values from 0 to 31, as said below
Outputs:
- clip_grad: float32 [8192, 1024], P(('dp', 'grp'))
- group_loss: float32 [32], P('grp')
The draws below stay inside these ranges and needn't reach their ends.
Inputs may be any that keep to these rules, and one draw needn't show every extreme that they name: `clip_group`: every group has at least one clip. `caption_group`: every group has at least two captions.
All inputs are finite; a program needn't handle non-finite values.
Results may differ from the reference program's by a relative error of at most 0.0028.
Values may be sent and summed in bfloat16 or wider, within the bound.
No kernel may reach another device: no remote copies, remote signals or barrier semaphores. Data moves between devices by JAX's collectives and lax.ppermute only.
A program may use at most 64 MiB of HBM per device.

```python
import math
import jax
import jax.numpy as jnp
from jax import lax

D = 1024
NCLIPS = 8192
NCAPS = 128
GROUPS = 32


def group_ids(key):
    keys = jax.random.split(jax.random.fold_in(key, 7), 4)
    clip_perm = jax.random.permutation(keys[0], NCLIPS)
    clip_rand = jax.random.randint(keys[1], (NCLIPS,), 0, GROUPS)
    clip_ids = jnp.where(clip_perm < GROUPS, clip_perm, clip_rand).astype(jnp.int32)
    cap_perm = jax.random.permutation(keys[2], NCAPS)
    cap_rand = jax.random.randint(keys[3], (NCAPS,), 0, GROUPS)
    cap_ids = jnp.where(cap_perm < 2 * GROUPS, cap_perm % GROUPS, cap_rand).astype(jnp.int32)
    return (clip_ids, cap_ids)


def embeddings(key):
    keys = jax.random.split(jax.random.fold_in(key, 11), 2)
    clip_vals = jnp.clip(jax.random.normal(keys[0], (NCLIPS, D), jnp.float32), -4.0, 4.0)
    cap_vals = jnp.clip(jax.random.normal(keys[1], (NCAPS, D), jnp.float32), -4.0, 4.0)
    return (clip_vals, cap_vals)


def draw_clips(key, part):
    return embeddings(key)[0].astype(jnp.bfloat16)


def draw_captions(key, part):
    return embeddings(key)[1].astype(jnp.bfloat16)


def draw_clip_group(key, part):
    return group_ids(key)[0]


def draw_caption_group(key, part):
    return group_ids(key)[1]


def setup_inputs(seed: int = 0) -> dict:
    key_list = jax.random.split(jax.random.key(seed), 5)
    clips = draw_clips(jax.random.fold_in(key_list[4], 71), 0)
    captions = draw_captions(jax.random.fold_in(key_list[4], 71), 0)
    clip_group = draw_clip_group(jax.random.fold_in(key_list[4], 71), 0)
    caption_group = draw_caption_group(jax.random.fold_in(key_list[4], 71), 0)
    return dict(clips=clips, captions=captions, clip_group=clip_group, caption_group=caption_group)


NEGATIVE = -1e+30

def block_stats(clip_block, group_block, captions, caption_group):
    factor = 3.0 / math.sqrt(D)
    scores = jnp.dot(clip_block, captions.T, preferred_element_type=jnp.float32) * factor
    row_max = lax.optimization_barrier(jnp.max(scores, axis=1))
    weights = jnp.exp(scores - row_max[:, None])
    row_sum = lax.optimization_barrier(jnp.sum(weights, axis=1))
    positive = group_block[:, None] == caption_group[None, :]
    masked = jnp.where(positive, scores, NEGATIVE)
    pos_max = lax.optimization_barrier(jnp.max(masked, axis=1))
    pos_weights = jnp.where(positive, jnp.exp(masked - pos_max[:, None]), 0.0)
    pos_sum = lax.optimization_barrier(jnp.sum(pos_weights, axis=1))
    all_part = jnp.dot(weights.astype(jnp.bfloat16), captions, preferred_element_type=jnp.float32)
    pos_part = jnp.dot(pos_weights.astype(jnp.bfloat16), captions, preferred_element_type=jnp.float32)
    return (row_max, row_sum, pos_max, pos_sum, all_part, pos_part)

def reference(clips, captions, clip_group, caption_group):
    block_rows = 1024 if NCLIPS % 1024 == 0 else NCLIPS
    blocks = NCLIPS // block_rows

    def one_block(block_pair):
        return block_stats(block_pair[0], block_pair[1], captions, caption_group)
    block_out = lax.map(one_block, (clips.reshape(blocks, block_rows, D), clip_group.reshape(blocks, block_rows)))
    flat_out = [member_stat.reshape((NCLIPS,) + member_stat.shape[2:]) for member_stat in block_out]
    row_max, row_sum, pos_max, pos_sum, all_part, pos_part = flat_out
    group_max = jnp.full((GROUPS,), NEGATIVE, jnp.float32).at[clip_group].max(row_max)
    pos_group_max = jnp.full((GROUPS,), NEGATIVE, jnp.float32).at[clip_group].max(pos_max)
    weight = jnp.exp(row_max - group_max[clip_group])
    pos_weight = jnp.exp(pos_max - pos_group_max[clip_group])
    denominator = jax.ops.segment_sum(weight * row_sum, clip_group, num_segments=GROUPS)
    numerator = jax.ops.segment_sum(pos_weight * pos_sum, clip_group, num_segments=GROUPS)
    group_loss = group_max + jnp.log(denominator) - (pos_group_max + jnp.log(numerator))
    gain_all = weight / denominator[clip_group]
    gain_pos = pos_weight / numerator[clip_group]
    clip_grad = NCLIPS / GROUPS * (gain_all[:, None] * all_part - gain_pos[:, None] * pos_part)
    return (clip_grad, group_loss)
```

```python
import math

import jax
import jax.numpy as jnp
from jax import lax
from jax.sharding import PartitionSpec as P

NEGATIVE = -1e30
AXES = ("dp", "grp")
ID_BASE = 256
ID_LANES = 128


def everywhere(block, devices):
    copies = jnp.broadcast_to(block[None], (devices,) + block.shape)
    return lax.all_to_all(copies, AXES, 0, 0)


def lookup(onehot, first_col, second_col):
    return jnp.dot(
        onehot, jnp.stack([first_col, second_col], axis=1), precision=lax.Precision.HIGHEST
    )


def group_totals(onehot, first_col, second_col):
    values = jnp.stack([first_col, second_col], axis=1)
    return lax.dot_general(
        onehot, values, (((0,), (0,)), ((), ())), precision=lax.Precision.HIGHEST
    )


def shards(clips, captions, clip_group, caption_group):
    clip_rows, feat_width = clips.shape
    devices = lax.axis_size("dp") * lax.axis_size("grp")
    groups = captions.shape[0] * devices // 4
    nclips_all = clip_rows * devices
    factor = 3.0 / math.sqrt(feat_width)

    digits = jnp.stack([caption_group // ID_BASE, caption_group % ID_BASE], axis=1)
    digits = jnp.pad(digits.astype(jnp.bfloat16), ((0, 0), (0, ID_LANES - 2)))
    packed = everywhere(jnp.concatenate([captions, digits], axis=1), devices)
    packed = packed.reshape(devices * captions.shape[0], feat_width + ID_LANES)
    caps = packed[:, :feat_width]
    ids = packed[:, feat_width : feat_width + 2].astype(jnp.int32)
    ids = ids[:, 0] * ID_BASE + ids[:, 1]

    scores = (
        lax.dot_general(clips, caps, (((1,), (1,)), ((), ())), preferred_element_type=jnp.float32)
        * factor
    )
    row_max = jnp.max(scores, axis=1)
    weights = jnp.exp(scores - row_max[:, None])
    row_sum = jnp.sum(weights, axis=1)
    positive = clip_group[:, None] == ids[None, :]
    masked = jnp.where(positive, scores, NEGATIVE)
    pos_max = jnp.max(masked, axis=1)
    pos_weights = jnp.where(positive, jnp.exp(masked - pos_max[:, None]), 0.0)
    pos_sum = jnp.sum(pos_weights, axis=1)
    all_part = jnp.dot(weights.astype(jnp.bfloat16), caps, preferred_element_type=jnp.float32)
    pos_part = jnp.dot(pos_weights.astype(jnp.bfloat16), caps, preferred_element_type=jnp.float32)

    member = clip_group[:, None] == jnp.arange(groups, dtype=jnp.int32)[None, :]
    onehot = member.astype(jnp.float32)
    local_top = jnp.max(jnp.where(member, row_max[:, None], NEGATIVE), axis=0)
    local_pos_top = jnp.max(jnp.where(member, pos_max[:, None], NEGATIVE), axis=0)
    picked_local = lookup(onehot, local_top, local_pos_top)
    local_lift = jnp.exp(row_max - picked_local[:, 0])
    local_pos_lift = jnp.exp(pos_max - picked_local[:, 1])
    group_sums = group_totals(onehot, local_lift * row_sum, local_pos_lift * pos_sum)

    stats = jnp.concatenate([local_top, group_sums[:, 0], local_pos_top, group_sums[:, 1]])
    stats = everywhere(stats.reshape(1, -1), devices).reshape(devices, 4, groups)
    top_all = jnp.max(stats[:, 0], axis=0)
    top_pos = jnp.max(stats[:, 2], axis=0)
    denominator = jnp.sum(stats[:, 1] * jnp.exp(stats[:, 0] - top_all[None]), axis=0)
    numerator = jnp.sum(stats[:, 3] * jnp.exp(stats[:, 2] - top_pos[None]), axis=0)

    picked = lookup(onehot, top_all, top_pos)
    factors = lookup(onehot, 1.0 / denominator, 1.0 / numerator)
    gain_all = jnp.exp(row_max - picked[:, 0]) * factors[:, 0]
    gain_pos = jnp.exp(pos_max - picked[:, 1]) * factors[:, 1]
    full_loss = top_all + jnp.log(denominator) - (top_pos + jnp.log(numerator))
    own_share = groups // lax.axis_size("grp")
    group_loss = lax.dynamic_slice_in_dim(full_loss, lax.axis_index("grp") * own_share, own_share)
    clip_grad = (nclips_all / groups) * (
        gain_all[:, None] * all_part - gain_pos[:, None] * pos_part
    )
    return (clip_grad, group_loss)


def solution(mesh):
    return jax.shard_map(
        shards,
        mesh=mesh,
        in_specs=(P(AXES, None), P(AXES, None), P(AXES), P(AXES)),
        out_specs=(P(AXES, None), P("grp")),
        check_vma=False,
    )
```

```python
import functools
import math

import jax
import jax.numpy as jnp
from jax import lax
from jax.experimental import pallas as pl
from jax.experimental.pallas import tpu as pltpu
from jax.sharding import PartitionSpec as P

NEGATIVE = -1e30
AXES = ("dp", "grp")
ID_BASE = 256
LANES = 128
VMEM = pl.BlockSpec(memory_space=pltpu.VMEM)


def score_kernel(
    factor, groups, clips_ref, mine_ref, other_ref, group_ref, stats_ref, lift_ref, all_ref, pos_ref, caps
):
    rows, width = clips_ref.shape
    half = mine_ref.shape[0]
    caps[:half, :] = mine_ref[...]
    caps[half:, :] = other_ref[...]

    weigh_digit = lax.broadcasted_iota(jnp.int32, (8, LANES), 1)
    weigh_digit = jnp.where(weigh_digit == 0, float(ID_BASE), jnp.where(weigh_digit == 1, 1.0, 0.0))
    ids = lax.dot_general(
        weigh_digit.astype(jnp.bfloat16),
        caps[:, width:],
        (((1,), (1,)), ((), ())),
        preferred_element_type=jnp.float32,
    )[:1, :]

    eye = lax.broadcasted_iota(jnp.int32, (LANES, LANES), 0) == lax.broadcasted_iota(
        jnp.int32, (LANES, LANES), 1
    )
    group_row = group_ref[...].astype(jnp.float32)
    group_col = jnp.concatenate(
        [
            jnp.sum(
                jnp.where(eye, group_row[:, start : start + LANES], 0.0), axis=1, keepdims=True
            )
            for start in range(0, rows, LANES)
        ],
        axis=0,
    )

    caps_now = caps[:, :width]
    scores = (
        lax.dot_general(
            clips_ref[...], caps_now, (((1,), (1,)), ((), ())), preferred_element_type=jnp.float32
        )
        * factor
    )
    positive = group_col == ids
    row_max = jnp.max(scores, axis=1, keepdims=True)
    weights = jnp.exp(scores - row_max)
    row_sum = jnp.sum(weights, axis=1, keepdims=True)
    masked = jnp.where(positive, scores, NEGATIVE)
    pos_max = jnp.max(masked, axis=1, keepdims=True)
    pos_weights = jnp.where(positive, jnp.exp(masked - pos_max), 0.0)
    pos_sum = jnp.sum(pos_weights, axis=1, keepdims=True)

    lane = lax.broadcasted_iota(jnp.int32, (1, 4 * groups), 1)
    member = group_col.astype(jnp.int32) == lax.rem(lane, groups)
    block = lane // groups
    is_all = block < 2
    tops = jnp.where(is_all, row_max, pos_max)
    local_top = jnp.max(jnp.where(member, tops, NEGATIVE), axis=0, keepdims=True)
    lifts = jnp.where(member, jnp.exp(jnp.where(member, tops - local_top, 0.0)), 0.0)
    sums = jnp.sum(lifts * jnp.where(is_all, row_sum, pos_sum), axis=0, keepdims=True)
    is_top = lax.rem(block, 2) == 0
    stats_ref[...] = jnp.broadcast_to(jnp.where(is_top, local_top, sums), stats_ref.shape)
    lift_ref[...] = jnp.where(is_top, lifts, 0.0)

    all_ref[...] = jnp.dot(
        weights.astype(jnp.bfloat16), caps_now, preferred_element_type=jnp.float32
    )
    pos_ref[...] = jnp.dot(
        pos_weights.astype(jnp.bfloat16), caps_now, preferred_element_type=jnp.float32
    )


def finish_kernel(
    scale, groups, chunk, stats_ref, local_ref, lift_ref, all_ref, pos_ref, grad_ref, loss_ref, out, sems
):
    lanes = 4 * groups
    stats = stats_ref[...]
    top = jnp.max(stats, axis=0, keepdims=True)
    lifted = stats * pltpu.roll(jnp.exp(stats - top), groups, 1)
    totals = jnp.broadcast_to(jnp.sum(lifted, axis=0, keepdims=True), (8, lanes))
    top = jnp.broadcast_to(top, (8, lanes))
    lane = lax.broadcasted_iota(jnp.int32, (8, lanes), 1)
    is_top = lax.rem(lane // groups, 2) == 0
    totals = jnp.where(is_top, pltpu.roll(totals, lanes - groups, 1), 1.0)
    local_top = jnp.broadcast_to(local_ref[:1, :], (8, lanes))
    gains = jnp.where(is_top, jnp.exp(local_top - top) / totals * scale, 0.0)[:1, :]
    is_all = lane[:1, :] < 2 * groups
    gains_all = jnp.where(is_all, gains, 0.0)
    gains_pos = jnp.where(is_all, 0.0, gains)

    rows = all_ref.shape[0]
    copies = []
    for index, start in enumerate(range(0, rows, chunk)):
        part = slice(start, start + chunk)
        lifts = lift_ref[part, :]
        gain_all = jnp.sum(lifts * gains_all, axis=1, keepdims=True)
        gain_pos = jnp.sum(lifts * gains_pos, axis=1, keepdims=True)
        out[part, :] = gain_all * all_ref[part, :] - gain_pos * pos_ref[part, :]
        copy = pltpu.make_async_copy(out.at[part, :], grad_ref.at[part, :], sems.at[index])
        copy.start()
        copies.append(copy)

    level = top + jnp.log(totals)
    loss = level - pltpu.roll(level, lanes - 2 * groups, 1)
    share = loss_ref.shape[1]
    offset = lax.axis_index("grp") * share
    loss_ref[...] = pltpu.roll(loss, lax.rem(lanes - offset, lanes), 1)[:1, :share]
    for copy in copies:
        copy.wait()


def shards(clips, captions, clip_group, caption_group):
    rows, width = clips.shape
    own_caps = captions.shape[0]
    grp = lax.axis_size("grp")
    devices = lax.axis_size("dp") * grp
    groups = own_caps * devices // 4
    factor = 3.0 / math.sqrt(width)

    digits = jnp.stack([caption_group // ID_BASE, caption_group % ID_BASE], axis=1)
    digits = jnp.pad(digits.astype(jnp.bfloat16), ((0, 0), (0, LANES - 2)))
    packed = jnp.concatenate([captions, digits], axis=1)
    halves = packed.reshape(2, own_caps // 2, width + LANES)
    halves = jnp.broadcast_to(halves[None], (devices // 2,) + halves.shape)
    halves = halves.reshape(devices, own_caps // 2, width + LANES)
    mine = lax.all_to_all(halves, AXES, 0, 0).reshape(-1, width + LANES)
    other = lax.ppermute(mine, "grp", [(i, i ^ 1) for i in range(grp)])

    grant = (6 << 20) + 24 * rows * own_caps * devices
    f32 = functools.partial(jax.ShapeDtypeStruct, dtype=jnp.float32)
    local, lifts, all_part, pos_part = pl.pallas_call(
        functools.partial(score_kernel, factor, groups),
        out_shape=[
            f32((devices, 4 * groups)),
            f32((rows, 4 * groups)),
            f32((rows, width)),
            f32((rows, width)),
        ],
        in_specs=[VMEM] * 4,
        out_specs=[VMEM] * 4,
        scratch_shapes=[pltpu.VMEM((own_caps * devices, width + LANES), jnp.bfloat16)],
        compiler_params=pltpu.CompilerParams(vmem_limit_bytes=grant),
        name="scores",
    )(clips, mine, other, clip_group.reshape(1, rows))

    stats = lax.all_to_all(local, AXES, 0, 0, tiled=True)

    chunk = rows // 8
    clip_grad, group_loss = pl.pallas_call(
        functools.partial(finish_kernel, rows * devices / groups, groups, chunk),
        out_shape=[f32((rows, width)), f32((1, groups // grp))],
        in_specs=[VMEM] * 5,
        out_specs=[pl.BlockSpec(memory_space=pl.ANY), VMEM],
        scratch_shapes=[
            pltpu.VMEM((rows, width), jnp.float32),
            pltpu.SemaphoreType.DMA((rows // chunk,)),
        ],
        compiler_params=pltpu.CompilerParams(vmem_limit_bytes=grant),
        name="finish",
    )(stats, local, lifts, all_part, pos_part)
    return (clip_grad, group_loss.reshape(-1))


def solution(mesh):
    return jax.shard_map(
        shards,
        mesh=mesh,
        in_specs=(P(AXES, None), P(AXES, None), P(AXES), P(AXES)),
        out_specs=(P(AXES, None), P("grp")),
        check_vma=False,
    )
```

```python
import functools
import math

import jax
import jax.numpy as jnp
from jax import lax
from jax.experimental import pallas as pl
from jax.experimental.pallas import tpu as pltpu
from jax.sharding import PartitionSpec as P

NEGATIVE = -1e30
AXES = ("dp", "grp")
ID_BITS = 8
ID_BASE = 1 << ID_BITS
LANES = 128
VMEM = pl.BlockSpec(memory_space=pltpu.VMEM)
HBM = pl.BlockSpec(memory_space=pltpu.HBM)


def score_kernel(
    factor, groups, clips_ref, mine_ref, other_ref, group_ref, stats_ref, lift_ref, all_ref, pos_ref, caps
):
    rows, width = clips_ref.shape
    half = mine_ref.shape[0]
    caps[:half, :] = mine_ref[...]
    caps[half:, :] = other_ref[...]

    weigh_digit = lax.broadcasted_iota(jnp.int32, (8, LANES), 1)
    weigh_digit = jnp.where(weigh_digit == 0, float(ID_BASE), jnp.where(weigh_digit == 1, 1.0, 0.0))
    ids = lax.dot_general(
        weigh_digit.astype(jnp.bfloat16),
        caps[:, width:],
        (((1,), (1,)), ((), ())),
        preferred_element_type=jnp.float32,
    )[:1, :]

    eye = lax.broadcasted_iota(jnp.int32, (LANES, LANES), 0) == lax.broadcasted_iota(
        jnp.int32, (LANES, LANES), 1
    )
    group_row = group_ref[...].astype(jnp.float32)
    group_col = jnp.concatenate(
        [
            jnp.sum(
                jnp.where(eye, group_row[:, start : start + LANES], 0.0), axis=1, keepdims=True
            )
            for start in range(0, rows, LANES)
        ],
        axis=0,
    )

    caps_now = caps[:, :width]
    scores = (
        lax.dot_general(
            clips_ref[...], caps_now, (((1,), (1,)), ((), ())), preferred_element_type=jnp.float32
        )
        * factor
    )
    positive = group_col == ids
    row_max = jnp.max(scores, axis=1, keepdims=True)
    weights = jnp.exp(scores - row_max)
    row_sum = jnp.sum(weights, axis=1, keepdims=True)
    masked = jnp.where(positive, scores, NEGATIVE)
    pos_max = jnp.max(masked, axis=1, keepdims=True)
    pos_weights = jnp.where(positive, jnp.exp(masked - pos_max), 0.0)
    pos_sum = jnp.sum(pos_weights, axis=1, keepdims=True)

    lane = lax.broadcasted_iota(jnp.int32, (1, 4 * groups), 1)
    member = group_col.astype(jnp.int32) == lax.rem(lane, groups)
    block = lane // groups
    is_all = block < 2
    tops = jnp.where(is_all, row_max, pos_max)
    local_top = jnp.max(jnp.where(member, tops, NEGATIVE), axis=0, keepdims=True)
    lifts = jnp.where(member, jnp.exp(jnp.where(member, tops - local_top, 0.0)), 0.0)
    sums = jnp.sum(lifts * jnp.where(is_all, row_sum, pos_sum), axis=0, keepdims=True)
    is_top = lax.rem(block, 2) == 0
    stats_ref[...] = jnp.broadcast_to(jnp.where(is_top, local_top, sums), stats_ref.shape)
    lift_ref[...] = jnp.where(is_top, lifts, 0.0)

    all_ref[...] = jnp.dot(
        weights.astype(jnp.bfloat16), caps_now, preferred_element_type=jnp.float32
    )
    pos_ref[...] = jnp.dot(
        pos_weights.astype(jnp.bfloat16), caps_now, preferred_element_type=jnp.float32
    )


def pack_kernel(ids_ref, caps_ref, packed_ref, caps, ids, sems):
    copies = [
        pltpu.make_async_copy(ids_ref, ids, sems.at[0]),
        pltpu.make_async_copy(caps_ref, caps, sems.at[1]),
    ]
    for copy in copies:
        copy.start()
    for copy in copies:
        copy.wait()
    own_caps, width = caps.shape
    half = own_caps // 2
    row = lax.broadcasted_iota(jnp.int32, (own_caps, LANES), 0)
    lane = lax.broadcasted_iota(jnp.int32, (own_caps, LANES), 1)
    digits = jnp.zeros((own_caps, LANES), jnp.int32)
    for index in range(own_caps):
        high = lax.shift_right_logical(ids[index], ID_BITS)
        low = jnp.bitwise_and(ids[index], ID_BASE - 1)
        here = jnp.where(lane == 0, high, jnp.where(lane == 1, low, 0))
        digits = jnp.where(row == index, here, digits)
    digits = digits.astype(jnp.float32).astype(jnp.bfloat16)
    for part in range(2):
        packed_ref[part, :, :width] = caps[part * half : (part + 1) * half, :]
        packed_ref[part, :, width:] = digits[part * half : (part + 1) * half, :]


def finish_kernel(
    scale,
    groups,
    chunk,
    stats_ref,
    local_ref,
    lift_ref,
    all_ref,
    pos_ref,
    grad_ref,
    loss_ref,
    out,
    loss_out,
    sems,
    loss_sem,
):
    lanes = 4 * groups
    stats = stats_ref[...]
    top = jnp.max(stats, axis=0, keepdims=True)
    lifted = stats * pltpu.roll(jnp.exp(stats - top), groups, 1)
    totals = jnp.broadcast_to(jnp.sum(lifted, axis=0, keepdims=True), (8, lanes))
    top = jnp.broadcast_to(top, (8, lanes))
    lane = lax.broadcasted_iota(jnp.int32, (8, lanes), 1)
    is_top = lax.rem(lane // groups, 2) == 0
    totals = jnp.where(is_top, pltpu.roll(totals, lanes - groups, 1), 1.0)
    local_top = jnp.broadcast_to(local_ref[:1, :], (8, lanes))
    gains = jnp.where(is_top, jnp.exp(local_top - top) / totals * scale, 0.0)[:1, :]
    is_all = lane[:1, :] < 2 * groups
    gains_all = jnp.where(is_all, gains, 0.0)
    gains_pos = jnp.where(is_all, 0.0, gains)

    level = top + jnp.log(totals)
    loss = level - pltpu.roll(level, lanes - 2 * groups, 1)
    share = loss_out.shape[1]
    offset = lax.axis_index("grp") * share
    loss_out[...] = pltpu.roll(loss, lax.rem(lanes - offset, lanes), 1)[:1, :share]
    loss_copy = pltpu.make_async_copy(loss_out, loss_ref, loss_sem)
    loss_copy.start()

    rows = all_ref.shape[0]
    copies = [loss_copy]
    for index, start in enumerate(range(0, rows, chunk)):
        part = slice(start, start + chunk)
        lifts = lift_ref[part, :]
        gain_all = jnp.sum(lifts * gains_all, axis=1, keepdims=True)
        gain_pos = jnp.sum(lifts * gains_pos, axis=1, keepdims=True)
        out[part, :] = gain_all * all_ref[part, :] - gain_pos * pos_ref[part, :]
        copy = pltpu.make_async_copy(out.at[part, :], grad_ref.at[part, :], sems.at[index])
        copy.start()
        copies.append(copy)

    for copy in copies:
        copy.wait()


def shards(clips, captions, clip_group, caption_group):
    rows, width = clips.shape
    own_caps = captions.shape[0]
    grp = lax.axis_size("grp")
    devices = lax.axis_size("dp") * grp
    groups = own_caps * devices // 4
    factor = 3.0 / math.sqrt(width)

    halves = pl.pallas_call(
        pack_kernel,
        out_shape=jax.ShapeDtypeStruct((2, own_caps // 2, width + LANES), captions.dtype),
        in_specs=[HBM] * 2,
        out_specs=VMEM,
        scratch_shapes=[
            pltpu.VMEM(captions.shape, captions.dtype),
            pltpu.SMEM(caption_group.shape, caption_group.dtype),
            pltpu.SemaphoreType.DMA((2,)),
        ],
        compiler_params=pltpu.CompilerParams(vmem_limit_bytes=1 << 20),
        name="pack",
    )(*[pltpu.with_memory_space_constraint(a, pltpu.HBM) for a in (caption_group, captions)])
    halves = jnp.broadcast_to(halves[None], (devices // 2,) + halves.shape)
    halves = halves.reshape(devices, own_caps // 2, width + LANES)
    mine = lax.all_to_all(halves, AXES, 0, 0).reshape(-1, width + LANES)
    other = lax.ppermute(mine, "grp", [(i, i ^ 1) for i in range(grp)])

    grant = (6 << 20) + 24 * rows * own_caps * devices
    f32 = functools.partial(jax.ShapeDtypeStruct, dtype=jnp.float32)
    local, lifts, all_part, pos_part = pl.pallas_call(
        functools.partial(score_kernel, factor, groups),
        out_shape=[
            f32((devices, 4 * groups)),
            f32((rows, 4 * groups)),
            f32((rows, width)),
            f32((rows, width)),
        ],
        in_specs=[VMEM] * 4,
        out_specs=[VMEM] * 4,
        scratch_shapes=[pltpu.VMEM((own_caps * devices, width + LANES), jnp.bfloat16)],
        compiler_params=pltpu.CompilerParams(vmem_limit_bytes=grant),
        name="scores",
    )(clips, mine, other, clip_group.reshape(1, rows))

    stats = lax.all_to_all(local, AXES, 0, 0, tiled=True)

    chunk = rows // 8
    clip_grad, group_loss = pl.pallas_call(
        functools.partial(finish_kernel, rows * devices / groups, groups, chunk),
        out_shape=[f32((rows, width)), f32((1, groups // grp))],
        in_specs=[VMEM] * 5,
        out_specs=[HBM, HBM],
        scratch_shapes=[
            pltpu.VMEM((rows, width), jnp.float32),
            pltpu.VMEM((1, groups // grp), jnp.float32),
            pltpu.SemaphoreType.DMA((rows // chunk,)),
            pltpu.SemaphoreType.DMA,
        ],
        compiler_params=pltpu.CompilerParams(vmem_limit_bytes=grant),
        name="finish",
    )(stats, local, lifts, all_part, pos_part)
    return (clip_grad, group_loss.reshape(-1))


def solution(mesh):
    return jax.shard_map(
        shards,
        mesh=mesh,
        in_specs=(P(AXES, None), P(AXES, None), P(AXES), P(AXES)),
        out_specs=(P(AXES, None), P("grp")),
        check_vma=False,
    )
```

```python
import functools
import math

import jax
import jax.numpy as jnp
from jax import lax
from jax.experimental import pallas as pl
from jax.experimental.pallas import tpu as pltpu
from jax.sharding import PartitionSpec as P

NEGATIVE = -1e30
AXES = ("dp", "grp")
ID_BITS = 8
ID_BASE = 1 << ID_BITS
LANES = 128
ROW_CHUNK = 128
VMEM = pl.BlockSpec(memory_space=pltpu.VMEM)
HBM = pl.BlockSpec(memory_space=pltpu.HBM)


def score_kernel(
    factor, groups, clips_ref, mine_ref, other_ref, group_ref, stats_ref, lift_ref, all_ref, pos_ref, caps
):
    rows, width = clips_ref.shape
    half = mine_ref.shape[0]
    caps[:half, :] = mine_ref[...]
    caps[half:, :] = other_ref[...]

    weigh_digit = lax.broadcasted_iota(jnp.int32, (8, LANES), 1)
    weigh_digit = jnp.where(weigh_digit == 0, float(ID_BASE), jnp.where(weigh_digit == 1, 1.0, 0.0))
    ids = lax.dot_general(
        weigh_digit.astype(jnp.bfloat16),
        caps[:, width:],
        (((1,), (1,)), ((), ())),
        preferred_element_type=jnp.float32,
    )[:1, :]

    eye = lax.broadcasted_iota(jnp.int32, (LANES, LANES), 0) == lax.broadcasted_iota(
        jnp.int32, (LANES, LANES), 1
    )
    group_row = group_ref[...].astype(jnp.float32)
    group_col = jnp.concatenate(
        [
            jnp.sum(
                jnp.where(eye, group_row[:, start : start + LANES], 0.0), axis=1, keepdims=True
            )
            for start in range(0, rows, LANES)
        ],
        axis=0,
    )

    caps_now = caps[:, :width]
    lane = lax.broadcasted_iota(jnp.int32, (1, 4 * groups), 1)
    block = lane // groups
    is_all = block < 2
    is_top = lax.rem(block, 2) == 0
    lane_group = lax.rem(lane, groups).astype(jnp.float32)

    parts = [slice(start, start + ROW_CHUNK) for start in range(0, rows, ROW_CHUNK)]
    top_list, total_list, member_list, weight_list = [], [], [], []
    local_top = None

    for part in parts:
        group_part = group_col[part]
        scores = (
            lax.dot_general(
                clips_ref[part, :],
                caps_now,
                (((1,), (1,)), ((), ())),
                preferred_element_type=jnp.float32,
            )
            * factor
        )
        positive = group_part == ids
        masked = jnp.where(positive, scores, NEGATIVE)
        row_max = jnp.max(scores, axis=1, keepdims=True)
        pos_max = jnp.max(masked, axis=1, keepdims=True)
        weights = jnp.exp(scores - row_max)
        pos_weights = jnp.exp(masked - pos_max)
        weight_list.append((weights.astype(jnp.bfloat16), pos_weights.astype(jnp.bfloat16)))
        row_sum = jnp.sum(weights, axis=1, keepdims=True)
        pos_sum = jnp.sum(pos_weights, axis=1, keepdims=True)
        member = group_part == lane_group
        top = jnp.where(member, jnp.where(is_all, row_max, pos_max), NEGATIVE)
        here = jnp.max(top, axis=0, keepdims=True)
        local_top = here if local_top is None else jnp.maximum(local_top, here)
        top_list.append(top)
        total_list.append((row_sum, pos_sum))
        member_list.append(member)
    for kind, ref in enumerate((all_ref, pos_ref)):
        for part, pair in zip(parts, weight_list):
            ref[part, :] = jnp.dot(pair[kind], caps_now, preferred_element_type=jnp.float32)
    sums = 0.0
    for index, part in enumerate(parts):
        lifts = jnp.where(member_list[index], jnp.exp(top_list[index] - local_top), 0.0)
        row_sum, pos_sum = total_list[index]
        sums = sums + jnp.sum(lifts * jnp.where(is_all, row_sum, pos_sum), axis=0, keepdims=True)
        lift_ref[part, :] = jnp.where(is_top, lifts, 0.0)
    stats_ref[...] = jnp.broadcast_to(jnp.where(is_top, local_top, sums), stats_ref.shape)


def pack_kernel(ids_ref, caps_ref, packed_ref, caps, ids, sems):
    copies = [
        pltpu.make_async_copy(ids_ref, ids, sems.at[0]),
        pltpu.make_async_copy(caps_ref, caps, sems.at[1]),
    ]
    for copy in copies:
        copy.start()
    for copy in copies:
        copy.wait()
    own_caps, width = caps.shape
    half = own_caps // 2
    row = lax.broadcasted_iota(jnp.int32, (own_caps, LANES), 0)
    lane = lax.broadcasted_iota(jnp.int32, (own_caps, LANES), 1)
    digits = jnp.zeros((own_caps, LANES), jnp.int32)
    for index in range(own_caps):
        high = lax.shift_right_logical(ids[index], ID_BITS)
        low = jnp.bitwise_and(ids[index], ID_BASE - 1)
        here = jnp.where(lane == 0, high, jnp.where(lane == 1, low, 0))
        digits = jnp.where(row == index, here, digits)
    digits = digits.astype(jnp.float32).astype(jnp.bfloat16)
    for part in range(2):
        packed_ref[part, :, :width] = caps[part * half : (part + 1) * half, :]
        packed_ref[part, :, width:] = digits[part * half : (part + 1) * half, :]


def finish_kernel(
    scale,
    groups,
    chunk,
    stats_ref,
    local_ref,
    lift_ref,
    all_ref,
    pos_ref,
    grad_ref,
    loss_ref,
    out,
    loss_out,
    sems,
    loss_sem,
):
    lanes = 4 * groups
    stats = stats_ref[...]
    top = jnp.max(stats, axis=0, keepdims=True)
    lifted = stats * pltpu.roll(jnp.exp(stats - top), groups, 1)
    totals = jnp.broadcast_to(jnp.sum(lifted, axis=0, keepdims=True), (8, lanes))
    top = jnp.broadcast_to(top, (8, lanes))
    lane = lax.broadcasted_iota(jnp.int32, (8, lanes), 1)
    is_top = lax.rem(lane // groups, 2) == 0
    totals = jnp.where(is_top, pltpu.roll(totals, lanes - groups, 1), 1.0)
    local_top = jnp.broadcast_to(local_ref[:1, :], (8, lanes))
    gains = jnp.where(is_top, jnp.exp(local_top - top) / totals * scale, 0.0)[:1, :]
    is_all = lane[:1, :] < 2 * groups
    gains_all = jnp.where(is_all, gains, 0.0)
    gains_pos = jnp.where(is_all, 0.0, gains)

    rows = all_ref.shape[0]
    copies = []
    for index, start in enumerate(range(0, rows, chunk)):
        part = slice(start, start + chunk)
        lifts = lift_ref[part, :]
        gain_all = jnp.sum(lifts * gains_all, axis=1, keepdims=True)
        gain_pos = jnp.sum(lifts * gains_pos, axis=1, keepdims=True)
        out[part, :] = gain_all * all_ref[part, :] - gain_pos * pos_ref[part, :]
        copy = pltpu.make_async_copy(out.at[part, :], grad_ref.at[part, :], sems.at[index])
        copy.start()
        copies.append(copy)

    level = top + jnp.log(totals)
    loss = level - pltpu.roll(level, lanes - 2 * groups, 1)
    share = loss_out.shape[1]
    offset = lax.axis_index("grp") * share
    loss_out[...] = pltpu.roll(loss, lax.rem(lanes - offset, lanes), 1)[:1, :share]
    loss_copy = pltpu.make_async_copy(loss_out, loss_ref, loss_sem)
    loss_copy.start()
    copies.append(loss_copy)

    for copy in copies:
        copy.wait()


def shards(clips, captions, clip_group, caption_group):
    rows, width = clips.shape
    own_caps = captions.shape[0]
    grp = lax.axis_size("grp")
    devices = lax.axis_size("dp") * grp
    groups = own_caps * devices // 4
    factor = 3.0 / math.sqrt(width)

    halves = pl.pallas_call(
        pack_kernel,
        out_shape=jax.ShapeDtypeStruct((2, own_caps // 2, width + LANES), captions.dtype),
        in_specs=[HBM] * 2,
        out_specs=VMEM,
        scratch_shapes=[
            pltpu.VMEM(captions.shape, captions.dtype),
            pltpu.SMEM(caption_group.shape, caption_group.dtype),
            pltpu.SemaphoreType.DMA((2,)),
        ],
        compiler_params=pltpu.CompilerParams(vmem_limit_bytes=1 << 20),
        name="pack",
    )(*[pltpu.with_memory_space_constraint(a, pltpu.HBM) for a in (caption_group, captions)])
    halves = jnp.broadcast_to(halves[None], (devices // 2,) + halves.shape)
    halves = halves.reshape(devices, own_caps // 2, width + LANES)
    mine = lax.all_to_all(halves, AXES, 0, 0).reshape(-1, width + LANES)
    other = lax.ppermute(mine, "grp", [(i, i ^ 1) for i in range(grp)])

    grant = (6 << 20) + 24 * rows * own_caps * devices
    f32 = functools.partial(jax.ShapeDtypeStruct, dtype=jnp.float32)
    local, lifts, all_part, pos_part = pl.pallas_call(
        functools.partial(score_kernel, factor, groups),
        out_shape=[
            f32((devices, 4 * groups)),
            f32((rows, 4 * groups)),
            f32((rows, width)),
            f32((rows, width)),
        ],
        in_specs=[VMEM] * 4,
        out_specs=[VMEM] * 4,
        scratch_shapes=[pltpu.VMEM((own_caps * devices, width + LANES), jnp.bfloat16)],
        compiler_params=pltpu.CompilerParams(vmem_limit_bytes=grant),
        name="scores",
    )(clips, mine, other, clip_group.reshape(1, rows))

    stats = lax.all_to_all(local, AXES, 0, 0, tiled=True)

    chunk = rows // 8
    clip_grad, group_loss = pl.pallas_call(
        functools.partial(finish_kernel, rows * devices / groups, groups, chunk),
        out_shape=[f32((rows, width)), f32((1, groups // grp))],
        in_specs=[VMEM] * 5,
        out_specs=[HBM, HBM],
        scratch_shapes=[
            pltpu.VMEM((rows, width), jnp.float32),
            pltpu.VMEM((1, groups // grp), jnp.float32),
            pltpu.SemaphoreType.DMA((rows // chunk,)),
            pltpu.SemaphoreType.DMA,
        ],
        compiler_params=pltpu.CompilerParams(vmem_limit_bytes=grant),
        name="finish",
    )(stats, local, lifts, all_part, pos_part)
    return (clip_grad, group_loss.reshape(-1))


def solution(mesh):
    return jax.shard_map(
        shards,
        mesh=mesh,
        in_specs=(P(AXES, None), P(AXES, None), P(AXES), P(AXES)),
        out_specs=(P(AXES, None), P("grp")),
        check_vma=False,
    )
```

```python
import functools
import math

import jax
import jax.numpy as jnp
from jax import lax
from jax.experimental import pallas as pl
from jax.experimental.pallas import tpu as pltpu
from jax.sharding import PartitionSpec as P

NEGATIVE = -1e30
AXES = ("dp", "grp")
ID_BITS = 8
ID_BASE = 1 << ID_BITS
LANES = 128
ROW_CHUNK = 128
VMEM = pl.BlockSpec(memory_space=pltpu.VMEM)
HBM = pl.BlockSpec(memory_space=pltpu.HBM)


def score_kernel(
    factor, groups, clips_ref, mine_ref, other_ref, group_ref, stats_ref, lift_ref, all_ref, pos_ref, caps
):
    rows, width = clips_ref.shape
    half = mine_ref.shape[0]
    caps[:half, :] = mine_ref[...]
    caps[half:, :] = other_ref[...]

    weigh_digit = lax.broadcasted_iota(jnp.int32, (8, LANES), 1)
    weigh_digit = jnp.where(weigh_digit == 0, float(ID_BASE), jnp.where(weigh_digit == 1, 1.0, 0.0))
    ids = lax.dot_general(
        weigh_digit.astype(jnp.bfloat16),
        caps[:, width:],
        (((1,), (1,)), ((), ())),
        preferred_element_type=jnp.float32,
    )[:1, :]

    eye = lax.broadcasted_iota(jnp.int32, (LANES, LANES), 0) == lax.broadcasted_iota(
        jnp.int32, (LANES, LANES), 1
    )
    group_row = group_ref[...].astype(jnp.float32)
    group_col = jnp.concatenate(
        [
            jnp.sum(
                jnp.where(eye, group_row[:, start : start + LANES], 0.0), axis=1, keepdims=True
            )
            for start in range(0, rows, LANES)
        ],
        axis=0,
    )

    caps_now = caps[:, :width]
    lane = lax.broadcasted_iota(jnp.int32, (1, 4 * groups), 1)
    block = lane // groups
    is_all = block < 2
    is_top = lax.rem(block, 2) == 0
    lane_group = lax.rem(lane, groups).astype(jnp.float32)

    parts = [slice(start, start + ROW_CHUNK) for start in range(0, rows, ROW_CHUNK)]
    top_list, total_list, member_list, weight_list = [], [], [], []
    local_top = None

    for part in parts:
        group_part = group_col[part]
        scores = (
            lax.dot_general(
                clips_ref[part, :],
                caps_now,
                (((1,), (1,)), ((), ())),
                preferred_element_type=jnp.float32,
            )
            * factor
        )
        positive = group_part == ids
        masked = jnp.where(positive, scores, NEGATIVE)
        row_max = jnp.max(scores, axis=1, keepdims=True)
        pos_max = jnp.max(masked, axis=1, keepdims=True)
        weights = jnp.exp(scores - row_max)
        pos_weights = jnp.exp(masked - pos_max)
        weight_list.append((weights.astype(jnp.bfloat16), pos_weights.astype(jnp.bfloat16)))
        row_sum = jnp.sum(weights, axis=1, keepdims=True)
        pos_sum = jnp.sum(pos_weights, axis=1, keepdims=True)
        member = group_part == lane_group
        top = jnp.where(member, jnp.where(is_all, row_max, pos_max), NEGATIVE)
        here = jnp.max(top, axis=0, keepdims=True)
        local_top = here if local_top is None else jnp.maximum(local_top, here)
        top_list.append(top)
        total_list.append((row_sum, pos_sum))
        member_list.append(member)
    for kind, ref in enumerate((all_ref, pos_ref)):
        for part, pair in zip(parts, weight_list):
            ref[part, :] = jnp.dot(pair[kind], caps_now, preferred_element_type=jnp.float32)
    sums = 0.0
    for index, part in enumerate(parts):
        lifts = jnp.where(member_list[index], jnp.exp(top_list[index] - local_top), 0.0)
        row_sum, pos_sum = total_list[index]
        sums = sums + jnp.sum(lifts * jnp.where(is_all, row_sum, pos_sum), axis=0, keepdims=True)
        lift_ref[part, :] = jnp.where(is_top, 0.0, lifts)
    stats_ref[...] = jnp.broadcast_to(jnp.where(is_top, local_top, sums), stats_ref.shape)


def pack_kernel(ids_ref, caps_ref, packed_ref, caps, ids, sems):
    copies = [
        pltpu.make_async_copy(ids_ref, ids, sems.at[0]),
        pltpu.make_async_copy(caps_ref, caps, sems.at[1]),
    ]
    for copy in copies:
        copy.start()
    for copy in copies:
        copy.wait()
    own_caps, width = caps.shape
    half = own_caps // 2
    row = lax.broadcasted_iota(jnp.int32, (own_caps, LANES), 0)
    lane = lax.broadcasted_iota(jnp.int32, (own_caps, LANES), 1)
    digits = jnp.zeros((own_caps, LANES), jnp.int32)
    for index in range(own_caps):
        high = lax.shift_right_logical(ids[index], ID_BITS)
        low = jnp.bitwise_and(ids[index], ID_BASE - 1)
        here = jnp.where(lane == 0, high, jnp.where(lane == 1, low, 0))
        digits = jnp.where(row == index, here, digits)
    digits = digits.astype(jnp.float32).astype(jnp.bfloat16)
    for part in range(2):
        packed_ref[part, :, :width] = caps[part * half : (part + 1) * half, :]
        packed_ref[part, :, width:] = digits[part * half : (part + 1) * half, :]


def finish_kernel(
    scale,
    groups,
    chunk,
    stats_ref,
    local_ref,
    lift_ref,
    all_ref,
    pos_ref,
    grad_ref,
    loss_ref,
    out,
    loss_out,
    sems,
    loss_sem,
):
    lanes = 4 * groups
    devices = stats_ref.shape[0]
    stats = stats_ref[...]
    top = jnp.max(stats, axis=0, keepdims=True)
    lifts = jnp.exp(jnp.concatenate([stats, local_ref[:8, :]], axis=0) - top)
    lifts = pltpu.roll(lifts, groups, 1)
    totals = jnp.sum(stats * lifts[:devices], axis=0, keepdims=True)
    lane = lax.broadcasted_iota(jnp.int32, (1, lanes), 1)
    is_sum = lax.rem(lane // groups, 2) == 1
    totals = jnp.where(is_sum, totals, 1.0)
    gains = jnp.where(is_sum, lifts[devices : devices + 1] * (scale / totals), 0.0)
    is_all = lane < 2 * groups
    gains_all = jnp.where(is_all, gains, 0.0)
    gains_pos = jnp.where(is_all, 0.0, gains)

    rows = all_ref.shape[0]
    copies = []
    for index, start in enumerate(range(0, rows, chunk)):
        part = slice(start, start + chunk)
        own = lift_ref[part, :]
        gain_all = jnp.sum(own * gains_all, axis=1, keepdims=True)
        gain_pos = jnp.sum(own * gains_pos, axis=1, keepdims=True)
        out[part, :] = gain_all * all_ref[part, :] - gain_pos * pos_ref[part, :]
        copy = pltpu.make_async_copy(out.at[part, :], grad_ref.at[part, :], sems.at[index])
        copy.start()
        copies.append(copy)

    level = pltpu.roll(jnp.broadcast_to(top, (8, lanes)), groups, 1) + jnp.log(totals)
    loss = level - pltpu.roll(level, lanes - 2 * groups, 1)
    share = loss_out.shape[1]
    first = groups + lax.axis_index("grp") * share
    loss_out[...] = pltpu.roll(loss, lanes - first, 1)[:1, :share]
    loss_copy = pltpu.make_async_copy(loss_out, loss_ref, loss_sem)
    loss_copy.start()
    copies.append(loss_copy)

    for copy in copies:
        copy.wait()


def shards(clips, captions, clip_group, caption_group):
    rows, width = clips.shape
    own_caps = captions.shape[0]
    grp = lax.axis_size("grp")
    devices = lax.axis_size("dp") * grp
    groups = own_caps * devices // 4
    factor = 3.0 / math.sqrt(width)

    halves = pl.pallas_call(
        pack_kernel,
        out_shape=jax.ShapeDtypeStruct((2, own_caps // 2, width + LANES), captions.dtype),
        in_specs=[HBM] * 2,
        out_specs=VMEM,
        scratch_shapes=[
            pltpu.VMEM(captions.shape, captions.dtype),
            pltpu.SMEM(caption_group.shape, caption_group.dtype),
            pltpu.SemaphoreType.DMA((2,)),
        ],
        compiler_params=pltpu.CompilerParams(vmem_limit_bytes=1 << 20),
        name="pack",
    )(*[pltpu.with_memory_space_constraint(a, pltpu.HBM) for a in (caption_group, captions)])
    halves = jnp.broadcast_to(halves[None], (devices // 2,) + halves.shape)
    halves = halves.reshape(devices, own_caps // 2, width + LANES)
    mine = lax.all_to_all(halves, AXES, 0, 0).reshape(-1, width + LANES)
    other = lax.ppermute(mine, "grp", [(i, i ^ 1) for i in range(grp)])

    grant = (6 << 20) + 24 * rows * own_caps * devices
    f32 = functools.partial(jax.ShapeDtypeStruct, dtype=jnp.float32)
    local, lifts, all_part, pos_part = pl.pallas_call(
        functools.partial(score_kernel, factor, groups),
        out_shape=[
            f32((devices, 4 * groups)),
            f32((rows, 4 * groups)),
            f32((rows, width)),
            f32((rows, width)),
        ],
        in_specs=[VMEM] * 4,
        out_specs=[VMEM] * 4,
        scratch_shapes=[pltpu.VMEM((own_caps * devices, width + LANES), jnp.bfloat16)],
        compiler_params=pltpu.CompilerParams(vmem_limit_bytes=grant),
        name="scores",
    )(clips, mine, other, clip_group.reshape(1, rows))

    stats = lax.all_to_all(local, AXES, 0, 0, tiled=True)

    chunk = rows // 8
    clip_grad, group_loss = pl.pallas_call(
        functools.partial(finish_kernel, rows * devices / groups, groups, chunk),
        out_shape=[f32((rows, width)), f32((1, groups // grp))],
        in_specs=[VMEM] * 5,
        out_specs=[HBM, HBM],
        scratch_shapes=[
            pltpu.VMEM((rows, width), jnp.float32),
            pltpu.VMEM((1, groups // grp), jnp.float32),
            pltpu.SemaphoreType.DMA((rows // chunk,)),
            pltpu.SemaphoreType.DMA,
        ],
        compiler_params=pltpu.CompilerParams(vmem_limit_bytes=grant),
        name="finish",
    )(stats, local, lifts, all_part, pos_part)
    return (clip_grad, group_loss.reshape(-1))


def solution(mesh):
    return jax.shard_map(
        shards,
        mesh=mesh,
        in_specs=(P(AXES, None), P(AXES, None), P(AXES), P(AXES)),
        out_specs=(P(AXES, None), P("grp")),
        check_vma=False,
    )
```

```python
import functools
import math

import jax
import jax.numpy as jnp
from jax import lax
from jax.experimental import pallas as pl
from jax.experimental.pallas import tpu as pltpu
from jax.sharding import PartitionSpec as P

NEGATIVE = -1e30
AXES = ("dp", "grp")
ID_BITS = 8
ID_BASE = 1 << ID_BITS
LANES = 128
ROW_CHUNK = 128
VMEM = pl.BlockSpec(memory_space=pltpu.VMEM)
ANY = pl.BlockSpec(memory_space=pl.ANY)
HBM = pl.BlockSpec(memory_space=pltpu.HBM)


def in_hbm(array):
    return pltpu.with_memory_space_constraint(array, pltpu.HBM)


def score_kernel(
    factor, groups, clips_ref, mine_ref, other_ref, group_ref, stats_ref, lift_ref, all_ref, pos_ref, caps
):
    rows, width = clips_ref.shape
    half = mine_ref.shape[0]
    caps[:half, :] = mine_ref[...]
    caps[half:, :] = other_ref[...]

    weigh_digit = lax.broadcasted_iota(jnp.int32, (8, LANES), 1)
    weigh_digit = jnp.where(weigh_digit == 0, float(ID_BASE), jnp.where(weigh_digit == 1, 1.0, 0.0))
    ids = lax.dot_general(
        weigh_digit.astype(jnp.bfloat16),
        caps[:, width:],
        (((1,), (1,)), ((), ())),
        preferred_element_type=jnp.float32,
    )[:1, :]

    eye = lax.broadcasted_iota(jnp.int32, (LANES, LANES), 0) == lax.broadcasted_iota(
        jnp.int32, (LANES, LANES), 1
    )
    group_row = group_ref[...].astype(jnp.float32)
    group_col = jnp.concatenate(
        [
            jnp.sum(
                jnp.where(eye, group_row[:, start : start + LANES], 0.0), axis=1, keepdims=True
            )
            for start in range(0, rows, LANES)
        ],
        axis=0,
    )

    caps_now = caps[:, :width]
    lane = lax.broadcasted_iota(jnp.int32, (1, 4 * groups), 1)
    block = lane // groups
    is_all = block < 2
    is_top = lax.rem(block, 2) == 0
    lane_group = lax.rem(lane, groups).astype(jnp.float32)

    parts = [slice(start, start + ROW_CHUNK) for start in range(0, rows, ROW_CHUNK)]
    top_list, total_list, member_list, weight_list = [], [], [], []
    local_top = None

    for part in parts:
        group_part = group_col[part]
        scores = (
            lax.dot_general(
                clips_ref[part, :],
                caps_now,
                (((1,), (1,)), ((), ())),
                preferred_element_type=jnp.float32,
            )
            * factor
        )
        positive = group_part == ids
        masked = jnp.where(positive, scores, NEGATIVE)
        row_max = jnp.max(scores, axis=1, keepdims=True)
        pos_max = jnp.max(masked, axis=1, keepdims=True)
        weights = jnp.exp(scores - row_max)
        pos_weights = jnp.exp(masked - pos_max)
        weight_list.append((weights.astype(jnp.bfloat16), pos_weights.astype(jnp.bfloat16)))
        row_sum = jnp.sum(weights, axis=1, keepdims=True)
        pos_sum = jnp.sum(pos_weights, axis=1, keepdims=True)
        member = group_part == lane_group
        top = jnp.where(member, jnp.where(is_all, row_max, pos_max), NEGATIVE)
        here = jnp.max(top, axis=0, keepdims=True)
        local_top = here if local_top is None else jnp.maximum(local_top, here)
        top_list.append(top)
        total_list.append((row_sum, pos_sum))
        member_list.append(member)
    for kind, ref in enumerate((all_ref, pos_ref)):
        for part, pair in zip(parts, weight_list):
            ref[part, :] = jnp.dot(pair[kind], caps_now, preferred_element_type=jnp.float32)
    sums = 0.0
    for index, part in enumerate(parts):
        lifts = jnp.where(member_list[index], jnp.exp(top_list[index] - local_top), 0.0)
        row_sum, pos_sum = total_list[index]
        sums = sums + jnp.sum(lifts * jnp.where(is_all, row_sum, pos_sum), axis=0, keepdims=True)
        lift_ref[part, :] = jnp.where(is_top, 0.0, lifts)
    stats_ref[...] = jnp.broadcast_to(jnp.where(is_top, local_top, sums), stats_ref.shape)


def fetch_kernel(clips_ref, group_ref, after_ref, clips_out, group_out, sems):
    copies = [
        pltpu.make_async_copy(clips_ref, clips_out, sems.at[0]),
        pltpu.make_async_copy(group_ref, group_out, sems.at[1]),
    ]
    for copy in copies:
        copy.start()
    for copy in copies:
        copy.wait()


def pack_kernel(ids_ref, caps_ref, packed_ref, caps, ids, sems):
    copies = [
        pltpu.make_async_copy(ids_ref, ids, sems.at[0]),
        pltpu.make_async_copy(caps_ref, caps, sems.at[1]),
    ]
    for copy in copies:
        copy.start()
    for copy in copies:
        copy.wait()
    own_caps, width = caps.shape
    half = own_caps // 2
    row = lax.broadcasted_iota(jnp.int32, (own_caps, LANES), 0)
    lane = lax.broadcasted_iota(jnp.int32, (own_caps, LANES), 1)
    digits = jnp.zeros((own_caps, LANES), jnp.int32)
    for index in range(own_caps):
        high = lax.shift_right_logical(ids[index], ID_BITS)
        low = jnp.bitwise_and(ids[index], ID_BASE - 1)
        here = jnp.where(lane == 0, high, jnp.where(lane == 1, low, 0))
        digits = jnp.where(row == index, here, digits)
    digits = digits.astype(jnp.float32).astype(jnp.bfloat16)
    for part in range(2):
        packed_ref[part, :, :width] = caps[part * half : (part + 1) * half, :]
        packed_ref[part, :, width:] = digits[part * half : (part + 1) * half, :]


def finish_kernel(
    scale,
    groups,
    chunk,
    stats_ref,
    local_ref,
    lift_ref,
    all_ref,
    pos_ref,
    grad_ref,
    loss_ref,
    out,
    loss_out,
    sems,
    loss_sem,
):
    lanes = 4 * groups
    devices = stats_ref.shape[0]
    stats = stats_ref[...]
    top = jnp.max(stats, axis=0, keepdims=True)
    lifts = jnp.exp(jnp.concatenate([stats, local_ref[:8, :]], axis=0) - top)
    lifts = pltpu.roll(lifts, groups, 1)
    totals = jnp.sum(stats * lifts[:devices], axis=0, keepdims=True)
    lane = lax.broadcasted_iota(jnp.int32, (1, lanes), 1)
    is_sum = lax.rem(lane // groups, 2) == 1
    totals = jnp.where(is_sum, totals, 1.0)
    gains = jnp.where(is_sum, lifts[devices : devices + 1] * (scale / totals), 0.0)
    is_all = lane < 2 * groups
    gains_all = jnp.where(is_all, gains, 0.0)
    gains_pos = jnp.where(is_all, 0.0, gains)

    rows = all_ref.shape[0]
    copies = []
    for index, start in enumerate(range(0, rows, chunk)):
        part = slice(start, start + chunk)
        own = lift_ref[part, :]
        gain_all = jnp.sum(own * gains_all, axis=1, keepdims=True)
        gain_pos = jnp.sum(own * gains_pos, axis=1, keepdims=True)
        out[part, :] = gain_all * all_ref[part, :] - gain_pos * pos_ref[part, :]
        copy = pltpu.make_async_copy(out.at[part, :], grad_ref.at[part, :], sems.at[index])
        copy.start()
        copies.append(copy)

    level = pltpu.roll(jnp.broadcast_to(top, (8, lanes)), groups, 1) + jnp.log(totals)
    loss = level - pltpu.roll(level, lanes - 2 * groups, 1)
    share = loss_out.shape[1]
    first = groups + lax.axis_index("grp") * share
    loss_out[...] = pltpu.roll(loss, lanes - first, 1)[:1, :share]
    loss_copy = pltpu.make_async_copy(loss_out, loss_ref, loss_sem)
    loss_copy.start()
    copies.append(loss_copy)

    for copy in copies:
        copy.wait()


def shards(clips, captions, clip_group, caption_group):
    rows, width = clips.shape
    own_caps = captions.shape[0]
    grp = lax.axis_size("grp")
    devices = lax.axis_size("dp") * grp
    groups = own_caps * devices // 4
    factor = 3.0 / math.sqrt(width)

    halves = pl.pallas_call(
        pack_kernel,
        out_shape=jax.ShapeDtypeStruct((2, own_caps // 2, width + LANES), captions.dtype),
        in_specs=[HBM] * 2,
        out_specs=VMEM,
        scratch_shapes=[
            pltpu.VMEM(captions.shape, captions.dtype),
            pltpu.SMEM(caption_group.shape, caption_group.dtype),
            pltpu.SemaphoreType.DMA((2,)),
        ],
        compiler_params=pltpu.CompilerParams(vmem_limit_bytes=1 << 20),
        name="pack",
    )(in_hbm(caption_group), in_hbm(captions))
    halves = jnp.broadcast_to(halves[None], (devices // 2,) + halves.shape)
    halves = halves.reshape(devices, own_caps // 2, width + LANES)
    mine = lax.all_to_all(halves, AXES, 0, 0).reshape(-1, width + LANES)
    other = lax.ppermute(mine, "grp", [(i, i ^ 1) for i in range(grp)])

    clips, group_row = pl.pallas_call(
        fetch_kernel,
        out_shape=[
            jax.ShapeDtypeStruct(clips.shape, clips.dtype),
            jax.ShapeDtypeStruct((1, rows), clip_group.dtype),
        ],
        in_specs=[HBM, HBM, ANY],
        out_specs=[VMEM] * 2,
        scratch_shapes=[pltpu.SemaphoreType.DMA((2,))],
        compiler_params=pltpu.CompilerParams(vmem_limit_bytes=1 << 20),
        cost_estimate=pl.CostEstimate(
            flops=0, bytes_accessed=4 * clips.size, transcendentals=0
        ),
        name="fetch",
    )(in_hbm(clips), in_hbm(clip_group.reshape(1, rows)), mine)
    grant = (6 << 20) + 24 * rows * own_caps * devices
    f32 = functools.partial(jax.ShapeDtypeStruct, dtype=jnp.float32)
    local, lifts, all_part, pos_part = pl.pallas_call(
        functools.partial(score_kernel, factor, groups),
        out_shape=[
            f32((devices, 4 * groups)),
            f32((rows, 4 * groups)),
            f32((rows, width)),
            f32((rows, width)),
        ],
        in_specs=[VMEM] * 4,
        out_specs=[VMEM] * 4,
        scratch_shapes=[pltpu.VMEM((own_caps * devices, width + LANES), jnp.bfloat16)],
        compiler_params=pltpu.CompilerParams(vmem_limit_bytes=grant),
        name="scores",
    )(clips, mine, other, group_row)

    stats = lax.all_to_all(local, AXES, 0, 0, tiled=True)

    chunk = rows // 8
    clip_grad, group_loss = pl.pallas_call(
        functools.partial(finish_kernel, rows * devices / groups, groups, chunk),
        out_shape=[f32((rows, width)), f32((1, groups // grp))],
        in_specs=[VMEM] * 5,
        out_specs=[HBM, HBM],
        scratch_shapes=[
            pltpu.VMEM((rows, width), jnp.float32),
            pltpu.VMEM((1, groups // grp), jnp.float32),
            pltpu.SemaphoreType.DMA((rows // chunk,)),
            pltpu.SemaphoreType.DMA,
        ],
        compiler_params=pltpu.CompilerParams(vmem_limit_bytes=grant),
        name="finish",
    )(stats, local, lifts, all_part, pos_part)
    return (clip_grad, group_loss.reshape(-1))


def solution(mesh):
    return jax.shard_map(
        shards,
        mesh=mesh,
        in_specs=(P(AXES, None), P(AXES, None), P(AXES), P(AXES)),
        out_specs=(P(AXES, None), P("grp")),
        check_vma=False,
    )
```

```python
import functools
import math

import jax
import jax.numpy as jnp
from jax import lax
from jax.experimental import pallas as pl
from jax.experimental.pallas import tpu as pltpu
from jax.sharding import PartitionSpec as P

NEGATIVE = -1e30
AXES = ("dp", "grp")
ID_BITS = 8
ID_BASE = 1 << ID_BITS
LANES = 128
ROW_CHUNK = 128
GRAD_COPIES = 4
VMEM = pl.BlockSpec(memory_space=pltpu.VMEM)
ANY = pl.BlockSpec(memory_space=pl.ANY)
HBM = pl.BlockSpec(memory_space=pltpu.HBM)


def in_hbm(array):
    return pltpu.with_memory_space_constraint(array, pltpu.HBM)


def score_kernel(
    factor, groups, clips_ref, mine_ref, other_ref, group_ref, stats_ref, lift_ref, all_ref, pos_ref, caps
):
    rows, width = clips_ref.shape
    half = mine_ref.shape[0]
    caps[:half, :] = mine_ref[...]
    caps[half:, :] = other_ref[...]

    weigh_digit = lax.broadcasted_iota(jnp.int32, (8, LANES), 1)
    weigh_digit = jnp.where(weigh_digit == 0, float(ID_BASE), jnp.where(weigh_digit == 1, 1.0, 0.0))
    ids = lax.dot_general(
        weigh_digit.astype(jnp.bfloat16),
        caps[:, width:],
        (((1,), (1,)), ((), ())),
        preferred_element_type=jnp.float32,
    )[:1, :]

    eye = lax.broadcasted_iota(jnp.int32, (LANES, LANES), 0) == lax.broadcasted_iota(
        jnp.int32, (LANES, LANES), 1
    )
    group_row = group_ref[...].astype(jnp.float32)
    group_col = jnp.concatenate(
        [
            jnp.sum(
                jnp.where(eye, group_row[:, start : start + LANES], 0.0), axis=1, keepdims=True
            )
            for start in range(0, rows, LANES)
        ],
        axis=0,
    )

    caps_now = caps[:, :width]
    lane = lax.broadcasted_iota(jnp.int32, (1, 4 * groups), 1)
    block = lane // groups
    is_all = block < 2
    is_top = lax.rem(block, 2) == 0
    lane_group = lax.rem(lane, groups).astype(jnp.float32)

    parts = [slice(start, start + ROW_CHUNK) for start in range(0, rows, ROW_CHUNK)]
    top_list, total_list, member_list, weight_list = [], [], [], []
    local_top = None

    for part in parts:
        group_part = group_col[part]
        scores = (
            lax.dot_general(
                clips_ref[part, :],
                caps_now,
                (((1,), (1,)), ((), ())),
                preferred_element_type=jnp.float32,
            )
            * factor
        )
        positive = group_part == ids
        masked = jnp.where(positive, scores, NEGATIVE)
        row_max = jnp.max(scores, axis=1, keepdims=True)
        pos_max = jnp.max(masked, axis=1, keepdims=True)
        weights = jnp.exp(scores - row_max)
        pos_weights = jnp.exp(masked - pos_max)
        weight_list.append((weights.astype(jnp.bfloat16), pos_weights.astype(jnp.bfloat16)))
        row_sum = jnp.sum(weights, axis=1, keepdims=True)
        pos_sum = jnp.sum(pos_weights, axis=1, keepdims=True)
        member = group_part == lane_group
        top = jnp.where(member, jnp.where(is_all, row_max, pos_max), NEGATIVE)
        here = jnp.max(top, axis=0, keepdims=True)
        local_top = here if local_top is None else jnp.maximum(local_top, here)
        top_list.append(top)
        total_list.append((row_sum, pos_sum))
        member_list.append(member)
    for kind, ref in enumerate((all_ref, pos_ref)):
        for part, pair in zip(parts, weight_list):
            ref[part, :] = jnp.dot(pair[kind], caps_now, preferred_element_type=jnp.float32)
    sums = 0.0
    for index, part in enumerate(parts):
        lifts = jnp.where(member_list[index], jnp.exp(top_list[index] - local_top), 0.0)
        row_sum, pos_sum = total_list[index]
        sums = sums + jnp.sum(lifts * jnp.where(is_all, row_sum, pos_sum), axis=0, keepdims=True)
        lift_ref[part, :] = jnp.where(is_top, 0.0, lifts)
    stats_ref[...] = jnp.broadcast_to(jnp.where(is_top, local_top, sums), stats_ref.shape)


def fetch_kernel(clips_ref, group_ref, after_ref, clips_out, group_out, sems):
    copies = [
        pltpu.make_async_copy(clips_ref, clips_out, sems.at[0]),
        pltpu.make_async_copy(group_ref, group_out, sems.at[1]),
    ]
    for copy in copies:
        copy.start()
    for copy in copies:
        copy.wait()


def pack_kernel(ids_ref, caps_ref, packed_ref, caps, ids, sems):
    copies = [
        pltpu.make_async_copy(ids_ref, ids, sems.at[0]),
        pltpu.make_async_copy(caps_ref, caps, sems.at[1]),
    ]
    for copy in copies:
        copy.start()
    for copy in copies:
        copy.wait()
    own_caps, width = caps.shape
    half = own_caps // 2
    row = lax.broadcasted_iota(jnp.int32, (own_caps, LANES), 0)
    lane = lax.broadcasted_iota(jnp.int32, (own_caps, LANES), 1)
    digits = jnp.zeros((own_caps, LANES), jnp.int32)
    for index in range(own_caps):
        high = lax.shift_right_logical(ids[index], ID_BITS)
        low = jnp.bitwise_and(ids[index], ID_BASE - 1)
        here = jnp.where(lane == 0, high, jnp.where(lane == 1, low, 0))
        digits = jnp.where(row == index, here, digits)
    digits = digits.astype(jnp.float32).astype(jnp.bfloat16)
    for part in range(2):
        packed_ref[part, :, :width] = caps[part * half : (part + 1) * half, :]
        packed_ref[part, :, width:] = digits[part * half : (part + 1) * half, :]


def finish_kernel(
    scale,
    groups,
    stats_ref,
    local_ref,
    lift_ref,
    all_ref,
    pos_ref,
    grad_ref,
    loss_ref,
    out,
    loss_out,
    sems,
    loss_sem,
):
    lanes = 4 * groups
    devices = stats_ref.shape[0]
    stats = stats_ref[...]
    top = jnp.max(stats, axis=0, keepdims=True)
    lifts = jnp.exp(jnp.concatenate([stats, local_ref[:8, :]], axis=0) - top)
    lifts = pltpu.roll(lifts, groups, 1)
    totals = jnp.sum(stats * lifts[:devices], axis=0, keepdims=True)
    lane = lax.broadcasted_iota(jnp.int32, (1, lanes), 1)
    is_sum = lax.rem(lane // groups, 2) == 1
    totals = jnp.where(is_sum, totals, 1.0)
    gains = jnp.where(is_sum, lifts[devices : devices + 1] * (scale / totals), 0.0)
    is_all = lane < 2 * groups
    gains_all = jnp.where(is_all, gains, 0.0)
    gains_pos = jnp.where(is_all, 0.0, gains)

    rows = all_ref.shape[0]
    copies = []
    bounds = [0, rows // 16, rows // 4, rows // 2, rows]
    for index, (start, stop) in enumerate(zip(bounds, bounds[1:])):
        part = slice(start, stop)
        own = lift_ref[part, :]
        gain_all = jnp.sum(own * gains_all, axis=1, keepdims=True)
        gain_pos = jnp.sum(own * gains_pos, axis=1, keepdims=True)
        out[part, :] = gain_all * all_ref[part, :] - gain_pos * pos_ref[part, :]
        copy = pltpu.make_async_copy(out.at[part, :], grad_ref.at[part, :], sems.at[index])
        copy.start()
        copies.append(copy)

    level = pltpu.roll(jnp.broadcast_to(top, (8, lanes)), groups, 1) + jnp.log(totals)
    loss = level - pltpu.roll(level, lanes - 2 * groups, 1)
    share = loss_out.shape[1]
    first = groups + lax.axis_index("grp") * share
    loss_out[...] = pltpu.roll(loss, lanes - first, 1)[:1, :share]
    loss_copy = pltpu.make_async_copy(loss_out, loss_ref, loss_sem)
    loss_copy.start()
    copies.append(loss_copy)

    for copy in copies:
        copy.wait()


def shards(clips, captions, clip_group, caption_group):
    rows, width = clips.shape
    own_caps = captions.shape[0]
    grp = lax.axis_size("grp")
    devices = lax.axis_size("dp") * grp
    groups = own_caps * devices // 4
    factor = 3.0 / math.sqrt(width)

    halves = pl.pallas_call(
        pack_kernel,
        out_shape=jax.ShapeDtypeStruct((2, own_caps // 2, width + LANES), captions.dtype),
        in_specs=[HBM] * 2,
        out_specs=VMEM,
        scratch_shapes=[
            pltpu.VMEM(captions.shape, captions.dtype),
            pltpu.SMEM(caption_group.shape, caption_group.dtype),
            pltpu.SemaphoreType.DMA((2,)),
        ],
        compiler_params=pltpu.CompilerParams(vmem_limit_bytes=1 << 20),
        name="pack",
    )(in_hbm(caption_group), in_hbm(captions))
    halves = jnp.broadcast_to(halves[None], (devices // 2,) + halves.shape)
    halves = halves.reshape(devices, own_caps // 2, width + LANES)
    mine = lax.all_to_all(halves, AXES, 0, 0).reshape(-1, width + LANES)
    other = lax.ppermute(mine, "grp", [(i, i ^ 1) for i in range(grp)])

    clips, group_row = pl.pallas_call(
        fetch_kernel,
        out_shape=[
            jax.ShapeDtypeStruct(clips.shape, clips.dtype),
            jax.ShapeDtypeStruct((1, rows), clip_group.dtype),
        ],
        in_specs=[HBM, HBM, ANY],
        out_specs=[VMEM] * 2,
        scratch_shapes=[pltpu.SemaphoreType.DMA((2,))],
        compiler_params=pltpu.CompilerParams(vmem_limit_bytes=1 << 20),
        cost_estimate=pl.CostEstimate(
            flops=0, bytes_accessed=4 * clips.size, transcendentals=0
        ),
        name="fetch",
    )(in_hbm(clips), in_hbm(clip_group.reshape(1, rows)), mine)
    grant = (6 << 20) + 24 * rows * own_caps * devices
    f32 = functools.partial(jax.ShapeDtypeStruct, dtype=jnp.float32)
    local, lifts, all_part, pos_part = pl.pallas_call(
        functools.partial(score_kernel, factor, groups),
        out_shape=[
            f32((devices, 4 * groups)),
            f32((rows, 4 * groups)),
            f32((rows, width)),
            f32((rows, width)),
        ],
        in_specs=[VMEM] * 4,
        out_specs=[VMEM] * 4,
        scratch_shapes=[pltpu.VMEM((own_caps * devices, width + LANES), jnp.bfloat16)],
        compiler_params=pltpu.CompilerParams(vmem_limit_bytes=grant),
        name="scores",
    )(clips, mine, other, group_row)

    stats = lax.all_to_all(local, AXES, 0, 0, tiled=True)

    clip_grad, group_loss = pl.pallas_call(
        functools.partial(finish_kernel, rows * devices / groups, groups),
        out_shape=[f32((rows, width)), f32((1, groups // grp))],
        in_specs=[VMEM] * 5,
        out_specs=[HBM, HBM],
        scratch_shapes=[
            pltpu.VMEM((rows, width), jnp.float32),
            pltpu.VMEM((1, groups // grp), jnp.float32),
            pltpu.SemaphoreType.DMA((GRAD_COPIES,)),
            pltpu.SemaphoreType.DMA,
        ],
        compiler_params=pltpu.CompilerParams(vmem_limit_bytes=grant),
        name="finish",
    )(stats, local, lifts, all_part, pos_part)
    return (clip_grad, group_loss.reshape(-1))


def solution(mesh):
    return jax.shard_map(
        shards,
        mesh=mesh,
        in_specs=(P(AXES, None), P(AXES, None), P(AXES), P(AXES)),
        out_specs=(P(AXES, None), P("grp")),
        check_vma=False,
    )
```

```python
import functools
import math

import jax
import jax.numpy as jnp
from jax import lax
from jax.experimental import pallas as pl
from jax.experimental.pallas import tpu as pltpu
from jax.sharding import PartitionSpec as P

NEGATIVE = -1e30
AXES = ("dp", "grp")
ID_BITS = 8
ID_BASE = 1 << ID_BITS
LANES = 128
ROW_CHUNK = 128
GRAD_COPIES = 4
VMEM = pl.BlockSpec(memory_space=pltpu.VMEM)
ANY = pl.BlockSpec(memory_space=pl.ANY)
HBM = pl.BlockSpec(memory_space=pltpu.HBM)


def in_hbm(array):
    return pltpu.with_memory_space_constraint(array, pltpu.HBM)


def score_kernel(
    factor, groups, clips_ref, mine_ref, other_ref, group_ref, stats_ref, lift_ref, all_ref, pos_ref
):
    rows, width = clips_ref.shape
    caps = jnp.concatenate([mine_ref[...], other_ref[...]], axis=0)

    weigh_digit = lax.broadcasted_iota(jnp.int32, (8, LANES), 1)
    weigh_digit = jnp.where(weigh_digit == 0, float(ID_BASE), jnp.where(weigh_digit == 1, 1.0, 0.0))
    ids = lax.dot_general(
        weigh_digit.astype(jnp.bfloat16),
        caps[:, width:],
        (((1,), (1,)), ((), ())),
        preferred_element_type=jnp.float32,
    )[:1, :]

    eye = lax.broadcasted_iota(jnp.int32, (LANES, LANES), 0) == lax.broadcasted_iota(
        jnp.int32, (LANES, LANES), 1
    )
    group_row = group_ref[...].astype(jnp.float32)
    group_col = jnp.concatenate(
        [
            jnp.sum(
                jnp.where(eye, group_row[:, start : start + LANES], 0.0), axis=1, keepdims=True
            )
            for start in range(0, rows, LANES)
        ],
        axis=0,
    )

    caps_now = caps[:, :width]
    lane = lax.broadcasted_iota(jnp.int32, (1, 4 * groups), 1)
    block = lane // groups
    is_all = block < 2
    is_top = lax.rem(block, 2) == 0
    lane_group = lax.rem(lane, groups).astype(jnp.float32)

    parts = [slice(start, start + ROW_CHUNK) for start in range(0, rows, ROW_CHUNK)]
    top_list, total_list, member_list, weight_list = [], [], [], []
    local_top = None

    for part in parts:
        group_part = group_col[part]
        scores = (
            lax.dot_general(
                clips_ref[part, :],
                caps_now,
                (((1,), (1,)), ((), ())),
                preferred_element_type=jnp.float32,
            )
            * factor
        )
        positive = group_part == ids
        masked = jnp.where(positive, scores, NEGATIVE)
        row_max = jnp.max(scores, axis=1, keepdims=True)
        pos_max = jnp.max(masked, axis=1, keepdims=True)
        weights = jnp.exp(scores - row_max)
        pos_weights = jnp.exp(masked - pos_max)
        weight_list.append((weights.astype(jnp.bfloat16), pos_weights.astype(jnp.bfloat16)))
        row_sum = jnp.sum(weights, axis=1, keepdims=True)
        pos_sum = jnp.sum(pos_weights, axis=1, keepdims=True)
        member = group_part == lane_group
        top = jnp.where(member, jnp.where(is_all, row_max, pos_max), NEGATIVE)
        here = jnp.max(top, axis=0, keepdims=True)
        local_top = here if local_top is None else jnp.maximum(local_top, here)
        top_list.append(top)
        total_list.append((row_sum, pos_sum))
        member_list.append(member)
    for kind, ref in enumerate((all_ref, pos_ref)):
        for part, pair in zip(parts, weight_list):
            ref[part, :] = jnp.dot(pair[kind], caps_now, preferred_element_type=jnp.float32)
    sums = 0.0
    for index, part in enumerate(parts):
        lifts = jnp.where(member_list[index], jnp.exp(top_list[index] - local_top), 0.0)
        row_sum, pos_sum = total_list[index]
        sums = sums + jnp.sum(lifts * jnp.where(is_all, row_sum, pos_sum), axis=0, keepdims=True)
        lift_ref[part, :] = jnp.where(is_top, 0.0, lifts)
    stats_ref[...] = jnp.broadcast_to(jnp.where(is_top, local_top, sums), stats_ref.shape)


def fetch_kernel(clips_ref, group_ref, after_ref, clips_out, group_out, sems):
    copies = [
        pltpu.make_async_copy(clips_ref, clips_out, sems.at[0]),
        pltpu.make_async_copy(group_ref, group_out, sems.at[1]),
    ]
    for copy in copies:
        copy.start()
    for copy in copies:
        copy.wait()


def pack_kernel(ids_ref, caps_ref, packed_ref, caps, ids, sems):
    copies = [
        pltpu.make_async_copy(ids_ref, ids, sems.at[0]),
        pltpu.make_async_copy(caps_ref, caps, sems.at[1]),
    ]
    for copy in copies:
        copy.start()
    for copy in copies:
        copy.wait()
    own_caps, width = caps.shape
    half = own_caps // 2
    row = lax.broadcasted_iota(jnp.int32, (own_caps, LANES), 0)
    lane = lax.broadcasted_iota(jnp.int32, (own_caps, LANES), 1)
    digits = jnp.zeros((own_caps, LANES), jnp.int32)
    for index in range(own_caps):
        high = lax.shift_right_logical(ids[index], ID_BITS)
        low = jnp.bitwise_and(ids[index], ID_BASE - 1)
        here = jnp.where(lane == 0, high, jnp.where(lane == 1, low, 0))
        digits = jnp.where(row == index, here, digits)
    digits = digits.astype(jnp.float32).astype(jnp.bfloat16)
    for part in range(2):
        packed_ref[part, :, :width] = caps[part * half : (part + 1) * half, :]
        packed_ref[part, :, width:] = digits[part * half : (part + 1) * half, :]


def finish_kernel(
    scale,
    groups,
    stats_ref,
    local_ref,
    lift_ref,
    all_ref,
    pos_ref,
    grad_ref,
    loss_ref,
    out,
    loss_out,
    sems,
    loss_sem,
):
    lanes = 4 * groups
    devices = stats_ref.shape[0]
    stats = stats_ref[...]
    top = jnp.max(stats, axis=0, keepdims=True)
    lifts = jnp.exp(jnp.concatenate([stats, local_ref[:8, :]], axis=0) - top)
    lifts = pltpu.roll(lifts, groups, 1)
    totals = jnp.sum(stats * lifts[:devices], axis=0, keepdims=True)
    lane = lax.broadcasted_iota(jnp.int32, (1, lanes), 1)
    is_sum = lax.rem(lane // groups, 2) == 1
    totals = jnp.where(is_sum, totals, 1.0)
    gains = jnp.where(is_sum, lifts[devices : devices + 1] * (scale / totals), 0.0)
    is_all = lane < 2 * groups
    gains_all = jnp.where(is_all, gains, 0.0)
    gains_pos = jnp.where(is_all, 0.0, gains)

    rows = all_ref.shape[0]
    copies = []
    bounds = [0, rows // 16, rows // 4, rows // 2, rows]
    for index, (start, stop) in enumerate(zip(bounds, bounds[1:])):
        part = slice(start, stop)
        own = lift_ref[part, :]
        gain_all = jnp.sum(own * gains_all, axis=1, keepdims=True)
        gain_pos = jnp.sum(own * gains_pos, axis=1, keepdims=True)
        out[part, :] = gain_all * all_ref[part, :] - gain_pos * pos_ref[part, :]
        copy = pltpu.make_async_copy(out.at[part, :], grad_ref.at[part, :], sems.at[index])
        copy.start()
        copies.append(copy)

    level = pltpu.roll(jnp.broadcast_to(top, (8, lanes)), groups, 1) + jnp.log(totals)
    loss = level - pltpu.roll(level, lanes - 2 * groups, 1)
    share = loss_out.shape[1]
    first = groups + lax.axis_index("grp") * share
    loss_out[...] = pltpu.roll(loss, lanes - first, 1)[:1, :share]
    loss_copy = pltpu.make_async_copy(loss_out, loss_ref, loss_sem)
    loss_copy.start()
    copies.append(loss_copy)

    for copy in copies:
        copy.wait()


def shards(clips, captions, clip_group, caption_group):
    rows, width = clips.shape
    own_caps = captions.shape[0]
    grp = lax.axis_size("grp")
    devices = lax.axis_size("dp") * grp
    groups = own_caps * devices // 4
    factor = 3.0 / math.sqrt(width)

    halves = pl.pallas_call(
        pack_kernel,
        out_shape=jax.ShapeDtypeStruct((2, own_caps // 2, width + LANES), captions.dtype),
        in_specs=[HBM] * 2,
        out_specs=VMEM,
        scratch_shapes=[
            pltpu.VMEM(captions.shape, captions.dtype),
            pltpu.SMEM(caption_group.shape, caption_group.dtype),
            pltpu.SemaphoreType.DMA((2,)),
        ],
        compiler_params=pltpu.CompilerParams(vmem_limit_bytes=1 << 20),
        name="pack",
    )(in_hbm(caption_group), in_hbm(captions))
    halves = jnp.broadcast_to(halves[None], (devices // 2,) + halves.shape)
    halves = halves.reshape(devices, own_caps // 2, width + LANES)
    mine = lax.all_to_all(halves, AXES, 0, 0).reshape(-1, width + LANES)
    other = lax.ppermute(mine, "grp", [(i, i ^ 1) for i in range(grp)])

    clips, group_row = pl.pallas_call(
        fetch_kernel,
        out_shape=[
            jax.ShapeDtypeStruct(clips.shape, clips.dtype),
            jax.ShapeDtypeStruct((1, rows), clip_group.dtype),
        ],
        in_specs=[HBM, HBM, ANY],
        out_specs=[VMEM] * 2,
        scratch_shapes=[pltpu.SemaphoreType.DMA((2,))],
        compiler_params=pltpu.CompilerParams(vmem_limit_bytes=1 << 20),
        cost_estimate=pl.CostEstimate(
            flops=0, bytes_accessed=4 * clips.size, transcendentals=0
        ),
        name="fetch",
    )(in_hbm(clips), in_hbm(clip_group.reshape(1, rows)), mine)
    grant = (6 << 20) + 24 * rows * own_caps * devices
    f32 = functools.partial(jax.ShapeDtypeStruct, dtype=jnp.float32)
    local, lifts, all_part, pos_part = pl.pallas_call(
        functools.partial(score_kernel, factor, groups),
        out_shape=[
            f32((devices, 4 * groups)),
            f32((rows, 4 * groups)),
            f32((rows, width)),
            f32((rows, width)),
        ],
        in_specs=[VMEM] * 4,
        out_specs=[VMEM] * 4,
        compiler_params=pltpu.CompilerParams(vmem_limit_bytes=grant),
        name="scores",
    )(clips, mine, other, group_row)

    stats = lax.all_to_all(local, AXES, 0, 0, tiled=True)

    clip_grad, group_loss = pl.pallas_call(
        functools.partial(finish_kernel, rows * devices / groups, groups),
        out_shape=[f32((rows, width)), f32((1, groups // grp))],
        in_specs=[VMEM] * 5,
        out_specs=[HBM, HBM],
        scratch_shapes=[
            pltpu.VMEM((rows, width), jnp.float32),
            pltpu.VMEM((1, groups // grp), jnp.float32),
            pltpu.SemaphoreType.DMA((GRAD_COPIES,)),
            pltpu.SemaphoreType.DMA,
        ],
        compiler_params=pltpu.CompilerParams(vmem_limit_bytes=grant),
        name="finish",
    )(stats, local, lifts, all_part, pos_part)
    return (clip_grad, group_loss.reshape(-1))


def solution(mesh):
    return jax.shard_map(
        shards,
        mesh=mesh,
        in_specs=(P(AXES, None), P(AXES, None), P(AXES), P(AXES)),
        out_specs=(P(AXES, None), P("grp")),
        check_vma=False,
    )
```
